32 devices in a mesh: grp: 2 (over x), seq: 8 (over z, y), head: 2 (over core).
Axes of the slice: x: 2, y: 2, z: 4, core: 2. Of those that a mesh axis runs over, the one named last changes fastest.
Arguments:
- q_nope: bfloat16 [8, 128, 128], P('grp', ('seq', 'head')), parts along dimension 0, may hold values from -6 to 6
- q_rope: bfloat16 [8, 128, 64], P('grp', ('seq', 'head')), parts along dimension 0, may hold values from -150 to 150
- w_uk: bfloat16 [128, 128, 512], P(('seq', 'head')), may hold values from -0.5 to 0.5
- w_uv: bfloat16 [128, 512, 128], P(('seq', 'head')), may hold values from -1 to 1
- cache: bfloat16 [8, 4096, 576], P('grp', 'seq'), parts along dimension 0, may hold values from -12 to 12
- lengths: int32 [8], P('grp'), parts along dimension 0, may hold values from 2048 to 4096, as said below
- selected: int32 [8, 8, 32], P('grp'), parts along dimension 0, may hold values from 0 to 63, as said below
Outputs:
- attended: bfloat16 [8, 128, 128], P('grp', ('seq', 'head')), parts along dimension 0
- bounds: float32 [8, 8, 64], P('grp', None, 'seq'), parts along dimension 0
The draws below stay inside these ranges and needn't reach their ends.
There are 2 independent parts, one for each index of `grp`. The reference program is written for one: setup_inputs(seed, part) draws one part's arguments, and reference() takes and returns one part's arrays. A program takes and returns all parts, laid end to end along the dimension named above; an argument that names none is the same for every part. Nothing has to cross between parts.
Inputs may be any that keep to these rules, and one draw needn't show every extreme that they name: `lengths`: some request has exactly 4096 cached tokens; every request has 2048 or more. `selected`: for each request and head group the 32 page numbers are distinct and below ceil(lengths[r] / 64); page 0 and the page of the request's last cached token are always among them.
All inputs are finite; a program needn't handle non-finite values.
Results may differ from the reference program's by a relative error of at most 0.0065.
Values may be sent and summed in bfloat16 or wider, within the bound.
A program may use at most 64 MiB of HBM per device.

```python
import jax
import jax.numpy as jnp
from jax import lax

H = 128
DN = 128
DR = 64
DL = 512
DV = 128
GH = 16
PAGE = 64
SEL = 32
R = 4
NG = 8
PAGES = 64
L = 4096


def shared_lengths(key):
    uniform_len = jax.random.randint(jax.random.fold_in(key, 11), (R,), SEL * PAGE, L + 1)
    longest = jax.random.randint(jax.random.fold_in(key, 12), (), 0, R)
    return jnp.where(jnp.arange(R) == longest, L, uniform_len).astype(jnp.int32)


def draw_lengths(key, part):
    return shared_lengths(key)


def draw_selected(key, part):
    request_len = shared_lengths(key)
    pages_used = (request_len + PAGE - 1) // PAGE
    subkeys = jax.random.split(jax.random.fold_in(key, 13), R * NG)

    def shuffle(subkey):
        return jax.random.permutation(subkey, PAGES)
    shuffled = jax.vmap(shuffle)(subkeys).reshape(R, NG, PAGES).astype(jnp.int32)
    page_number = jnp.arange(PAGES, dtype=jnp.int32)[None, None, :]
    ranking = jnp.where(page_number >= pages_used[:, None, None], shuffled + 2 * PAGES, shuffled)
    ranking = jnp.where(page_number == 0, -2, ranking)
    ranking = jnp.where(page_number == (pages_used - 1)[:, None, None], -1, ranking)
    ordering = jnp.argsort(ranking, axis=-1, stable=True)
    return ordering[:, :, :SEL].astype(jnp.int32)


def draw_cache(key, part):
    anchor = jax.random.fold_in(key, 31)
    latent = jnp.clip(jax.random.normal(jax.random.fold_in(anchor, 2), (R, L, DL), jnp.float32), -6.0, 6.0)
    rotary = jnp.clip(jax.random.normal(jax.random.fold_in(anchor, 3), (R, L, DR), jnp.float32), -6.0, 6.0)
    return jnp.concatenate([latent, rotary], axis=2).astype(jnp.bfloat16)


def draw_q_rope(key, part):
    anchor = jax.random.fold_in(key, 41)
    jitter = jax.random.normal(jax.random.fold_in(anchor, 1), (R, H, DR), jnp.float32)
    values = jnp.clip(jitter, -6.0, 6.0)
    return values.astype(jnp.bfloat16)


def levels(own_key, dims, pieces, low, high):
    def one(position, blocks):
        heights = jax.random.uniform(jax.random.fold_in(jax.random.fold_in(own_key, 6), position), (blocks,), jnp.float32, low / len(pieces), high / len(pieces))
        return jnp.repeat(jnp.exp(heights), dims[position] // blocks).reshape((-1,) + (1,) * (len(dims) - position - 1))

    factor_of = one(*pieces[0])
    for cut in pieces[1:]:
        factor_of = factor_of * one(*cut)
    return factor_of


def scatter_about(rng, shape, scale, most, shards=(), held_as=jnp.bfloat16):
    factor_of = levels(rng, shape, shards, -0.22, 0.18) if shards else 1.0
    values = jax.random.normal(rng, shape, jnp.float32) * scale * factor_of
    return jnp.minimum(jnp.maximum(values, -most), most).astype(held_as)


def setup_inputs(seed: int = 0, part: int = 0) -> dict:
    streams_of = jax.random.split(jax.random.key(seed), 8)
    part_splits = jax.random.split(jax.random.fold_in(streams_of[7], part), 8)
    return {
        "q_nope": scatter_about(part_splits[0], (R, H, DN), 1.0, 6.0, ((1, 16),)),
        "q_rope": draw_q_rope(jax.random.fold_in(jax.random.fold_in(streams_of[7], part), 71), part),
        "w_uk": scatter_about(streams_of[2], (H, DN, DL), DN ** -0.5, 0.5, ((0, 16),)),
        "w_uv": scatter_about(streams_of[3], (H, DL, DV), (DL // 16) ** -0.5, 1.0, ((0, 16),)),
        "cache": draw_cache(jax.random.fold_in(jax.random.fold_in(streams_of[7], part), 71), part),
        "lengths": draw_lengths(jax.random.fold_in(jax.random.fold_in(streams_of[7], part), 71), part),
        "selected": draw_selected(jax.random.fold_in(jax.random.fold_in(streams_of[7], part), 71), part),
    }


def reference(q_nope, q_rope, w_uk, w_uv, cache, lengths, selected):
    softmax_scale = (DN + DR) ** -0.5
    query_latent = jnp.einsum("rhn,hnl->rhl", q_nope.astype(jnp.float32), w_uk.astype(jnp.float32)).astype(jnp.bfloat16)
    absorbed = jnp.concatenate([query_latent, q_rope], axis=2)

    def per_request(inputs):
        query_rows, cache_rows, length, picks = inputs
        token_index = jnp.arange(PAGES * PAGE, dtype=jnp.int32).reshape(PAGES, PAGE)
        live_token = token_index < length
        live_page = live_token[:, 0]
        page_blocks = cache_rows.reshape(PAGES, PAGE, DL + DR).astype(jnp.float32)
        page_low = jnp.min(jnp.where(live_token[..., None], page_blocks, jnp.inf), axis=1)
        page_high = jnp.max(jnp.where(live_token[..., None], page_blocks, -jnp.inf), axis=1)
        page_low = jnp.where(live_page[:, None], page_low, 0.0)
        page_high = jnp.where(live_page[:, None], page_high, 0.0)
        middle = (page_low + page_high) * 0.5
        spread = (page_high - page_low) * 0.5
        query_float = query_rows.astype(jnp.float32)
        head_bound = softmax_scale * (
            jnp.dot(query_float, middle.T, precision=lax.Precision.HIGHEST)
            + jnp.dot(jnp.abs(query_float), spread.T, precision=lax.Precision.HIGHEST))
        group_bound = jnp.max(head_bound.reshape(NG, GH, PAGES), axis=1)
        group_bound = jnp.where(live_page[None, :], group_bound, 0.0)
        chosen = page_blocks[picks]
        chosen_live = live_token[picks]
        grouped = query_float.reshape(NG, GH, DL + DR)
        scores = jnp.einsum("gkd,gspd->gksp", grouped, chosen) * softmax_scale
        scores = jnp.where(chosen_live[:, None], scores, -1e30)
        page_top = jnp.max(scores, axis=3)
        weights = jnp.where(chosen_live[:, None], jnp.exp(scores - page_top[..., None]), 0.0).astype(jnp.bfloat16)
        weights = lax.optimization_barrier(weights).astype(jnp.float32)
        page_total = jnp.sum(weights, axis=3)
        page_weighted = jnp.einsum("gksp,gspl->gksl", weights, chosen[..., :DL])
        top = jnp.max(page_top, axis=2)
        factor = jnp.exp(page_top - top[..., None])
        total = jnp.sum(factor * page_total, axis=2)
        weighted = jnp.sum(factor[..., None] * page_weighted, axis=2)
        latent_out = (weighted / total[..., None]).astype(jnp.bfloat16).reshape(H, DL)
        return latent_out, group_bound

    latent_out, bounds = lax.map(per_request, (absorbed, cache, lengths, selected))
    attended = jnp.einsum("rhl,hlv->rhv", latent_out.astype(jnp.float32), w_uv.astype(jnp.float32)).astype(jnp.bfloat16)
    return (attended, bounds)
```

```python
import functools

import jax
import jax.numpy as jnp
from jax import lax
from jax.experimental import pallas as pl
from jax.experimental.pallas import tpu as pltpu
from jax.sharding import PartitionSpec as P

GH = 16
PAGE = 64
LOWEST = -1e30
FLOOR = -1e29
NT = (((1,), (1,)), ((), ()))


def kernel(
    n, hc, R, hb, T, DL, D, groups, scale,
    len_ref, qn_ref, qr_ref, sel_ref, wuk_hbm, wuv_hbm, cache_hbm,
    out_ref, bounds_ref,
    wuk, wuv, cache, gq, qf, pen, hi_s, lo_s, so, st, ro, rs, gb, gbr,
    in_sem, q_send, q_recv, o_send, o_recv, s_send, s_recv, b_send, b_recv,
):
    f32, bf16 = jnp.float32, jnp.bfloat16
    me = lax.axis_index("seq")
    hr = lax.axis_index("head")
    H = n * hb
    chunks = so.shape[0]
    RC = R // chunks
    pages = T // PAGE

    load_uk = pltpu.make_async_copy(wuk_hbm, wuk, in_sem.at[0])
    load_cache = [
        pltpu.make_async_copy(cache_hbm.at[r], cache.at[r], in_sem.at[2 + r]) for r in range(R)
    ]
    load_uv = pltpu.make_async_copy(wuv_hbm, wuv, in_sem.at[1])
    load_uk.start()
    for c in load_cache:
        c.start()
    load_uv.start()

    barrier = pltpu.get_barrier_semaphore()
    for k in range(1, n):
        pl.semaphore_signal(barrier, inc=1, device_id={"seq": lax.rem(me + k, n)})
    for k in range(1, hc):
        pl.semaphore_signal(barrier, inc=1, device_id={"head": lax.rem(hr + k, hc)})

    def spread(rows, width):
        which = lax.rem(lax.broadcasted_iota(jnp.int32, (R * hb, width), 0), hb)
        return jnp.concatenate(
            [jnp.where(which == h, rows, 0.0).astype(bf16) for h in range(hb)], axis=1
        )

    qn = jnp.concatenate([qn_ref[r].astype(f32) for r in range(R)], axis=0)
    qr = jnp.concatenate([qr_ref[r].astype(f32) for r in range(R)], axis=0)
    lhs = spread(qn, qn.shape[1])
    load_uk.wait()
    latent = jnp.dot(lhs, wuk[...].reshape(lhs.shape[1], DL), preferred_element_type=f32)
    gq[me, :, :DL] = latent.astype(bf16)
    gq[me, :, DL:] = qr.astype(bf16)

    pl.semaphore_wait(barrier, n - 1 + hc - 1)
    q_copies = []
    for k in range(1, n):
        c = pltpu.make_async_remote_copy(
            src_ref=gq.at[me], dst_ref=gq.at[me], send_sem=q_send.at[k], recv_sem=q_recv.at[k],
            device_id={"seq": lax.rem(me + k, n)},
        )
        c.start()
        q_copies.append(c)

    row_head = lax.broadcasted_iota(jnp.int32, (H, groups), 0)
    row_head = (lax.div(row_head, hb) * hc + hr) * hb + lax.rem(row_head, hb)
    hot = lax.div(row_head, GH) == lax.broadcasted_iota(jnp.int32, (H, groups), 1)
    hot_b = jnp.where(hot, 1.0, 0.0).astype(bf16)
    tok = me * T + lax.broadcasted_iota(jnp.int32, (groups, T), 1)
    page_of = lax.div(tok, PAGE)
    tok_col = me * T + lax.broadcasted_iota(jnp.int32, (T, 1), 0)
    page_col = (me * pages + lax.broadcasted_iota(jnp.int32, (pages, 1), 0)) * PAGE
    for r in range(R):
        length = len_ref[r]
        sel = sel_ref[r]
        hit = jnp.zeros((groups, T), f32)
        for k in range(sel.shape[1]):
            hit = jnp.where(sel[:, k:k + 1] == page_of, 1.0, hit)
        hit = jnp.where(tok < length, hit, 0.0)
        mask = jnp.dot(hot_b, hit.astype(bf16), preferred_element_type=f32)
        pen[r] = (1.0 - mask) * LOWEST
    for r in range(R):
        length = len_ref[r]
        load_cache[r].wait()
        x = cache[r].astype(f32)
        live = tok_col < length
        low = jnp.min(jnp.where(live, x, jnp.inf).reshape(pages, PAGE, D), axis=1)
        high = jnp.max(jnp.where(live, x, -jnp.inf).reshape(pages, PAGE, D), axis=1)
        live_page = page_col < length
        lo_s[r] = jnp.where(live_page, low, 0.0).astype(bf16)
        hi_s[r] = jnp.where(live_page, high, 0.0).astype(bf16)

    for c in q_copies:
        c.wait_recv()
    for s in range(n):
        block = gq[s].astype(f32)
        for r in range(R):
            qf[r, s * hb:(s + 1) * hb, :] = block[r * hb:(r + 1) * hb]

    lane = lax.broadcasted_iota(jnp.int32, (H, 128), 1)
    tops = jnp.zeros((H, 128), f32)
    sums = jnp.ones((H, 128), f32)
    o_copies = []
    for c in range(chunks):
        outs = []
        for r in range(c * RC, (c + 1) * RC):
            q = qf[r].astype(bf16)
            s = lax.dot_general(q, cache[r], NT, preferred_element_type=f32) * scale + pen[r]
            m = jnp.maximum(jnp.max(s, axis=1, keepdims=True), FLOOR)
            w = jnp.exp(s - m).astype(bf16)
            l = jnp.sum(w.astype(f32), axis=1, keepdims=True)
            outs.append(jnp.dot(w, cache[r, :, :DL], preferred_element_type=f32))
            tops = jnp.where(lane == r, m, tops)
            sums = jnp.where(lane == r, l, sums)
        for b in range(n):
            so[c, b] = jnp.concatenate(
                [o[b * hb:(b + 1) * hb] for o in outs], axis=0
            ).astype(bf16)
        if c == chunks - 1:
            for b in range(n):
                st[b, 0] = tops[b * hb:(b + 1) * hb]
                st[b, 1] = sums[b * hb:(b + 1) * hb]
        for k in range(1, n):
            to = lax.rem(me + k, n)
            cp = pltpu.make_async_remote_copy(
                src_ref=so.at[c, to], dst_ref=ro.at[c, me],
                send_sem=o_send.at[c, k], recv_sem=o_recv.at[c, k], device_id={"seq": to},
            )
            cp.start()
            o_copies.append(cp)
            if c == chunks - 1:
                cp = pltpu.make_async_remote_copy(
                    src_ref=st.at[to], dst_ref=rs.at[me],
                    send_sem=s_send.at[k], recv_sem=s_recv.at[k], device_id={"seq": to},
                )
                cp.start()
                o_copies.append(cp)

    parts = []
    for r in range(R):
        q = qf[r]
        above = jnp.maximum(q, 0.0).astype(bf16)
        below = jnp.minimum(q, 0.0).astype(bf16)
        parts.append(
            lax.dot_general(above, hi_s[r], NT, preferred_element_type=f32)
            + lax.dot_general(below, lo_s[r], NT, preferred_element_type=f32)
        )
    parts.append(jnp.zeros((H, 128 - R * pages), f32))
    head_bound = jnp.concatenate(parts, axis=1) * scale
    gb[...] = jnp.concatenate(
        [
            jnp.max(jnp.where(hot[:, g:g + 1], head_bound, LOWEST), axis=0, keepdims=True)
            for g in range(groups)
        ],
        axis=0,
    )
    b_copies = []
    for k in range(1, hc):
        cp = pltpu.make_async_remote_copy(
            src_ref=gb, dst_ref=gbr.at[k], send_sem=b_send.at[k], recv_sem=b_recv.at[k],
            device_id={"head": lax.rem(hr + k, hc)},
        )
        cp.start()
        b_copies.append(cp)
    for c in range(chunks):
        ro[c, me] = so[c, me]
    rs[me] = st[me]
    load_uv.wait()
    for cp in b_copies:
        cp.wait_recv()
    best = gb[...]
    for k in range(1, hc):
        best = jnp.maximum(best, gbr[k])
    page_row = (me * pages + lax.broadcasted_iota(jnp.int32, (groups, pages), 1)) * PAGE
    for r in range(R):
        bounds_ref[r] = jnp.where(
            page_row < len_ref[r], best[:, r * pages:(r + 1) * pages], 0.0
        )

    for cp in o_copies:
        cp.wait_recv()
    peak = rs[0, 0]
    for b in range(1, n):
        peak = jnp.maximum(peak, rs[b, 0])
    shares = [jnp.exp(rs[b, 0] - peak) for b in range(n)]
    total = shares[0] * rs[0, 1]
    for b in range(1, n):
        total += shares[b] * rs[b, 1]
    shares = [x / total for x in shares]
    rows = []
    for c in range(chunks):
        acc = [jnp.zeros((hb, DL), f32) for _ in range(RC)]
        for b in range(n):
            block = ro[c, b].astype(f32)
            for i in range(RC):
                r = c * RC + i
                acc[i] += shares[b][:, r:r + 1] * block[i * hb:(i + 1) * hb]
        rows += acc
    lhs = spread(jnp.concatenate(rows, axis=0), DL)
    res = jnp.dot(lhs, wuv[...].reshape(lhs.shape[1], wuv.shape[2]), preferred_element_type=f32)
    for r in range(R):
        out_ref[r] = res[r * hb:(r + 1) * hb].astype(bf16)
    for cp in q_copies + o_copies + b_copies:
        cp.wait_send()


def local(n, hc, q_nope, q_rope, w_uk, w_uv, cache, lengths, selected):
    R, hb, DN = q_nope.shape
    DL, DV = w_uk.shape[2], w_uv.shape[2]
    T, D = cache.shape[1:]
    groups = selected.shape[1]
    pages = T // PAGE
    H = n * hb
    chunks = 2 if R % 2 == 0 else 1
    scale = (DN + q_rope.shape[2]) ** (-0.5)
    f32, bf16 = jnp.float32, jnp.bfloat16
    V = pltpu.VMEM
    vm = pl.BlockSpec(memory_space=pltpu.VMEM)
    hbm = pl.BlockSpec(memory_space=pl.ANY)
    dma = pltpu.SemaphoreType.DMA
    return pl.pallas_call(
        functools.partial(kernel, n, hc, R, hb, T, DL, D, groups, scale),
        out_shape=(
            jax.ShapeDtypeStruct((R, hb, DV), bf16),
            jax.ShapeDtypeStruct((R, groups, pages), f32),
        ),
        in_specs=[pl.BlockSpec(memory_space=pltpu.SMEM), vm, vm, vm, hbm, hbm, hbm],
        out_specs=(vm, vm),
        scratch_shapes=[
            V((hb, DN, DL), bf16),
            V((hb, DL, DV), bf16),
            V((R, T, D), bf16),
            V((n, R * hb, D), bf16),
            V((R, H, D), f32),
            V((R, H, T), f32),
            V((R, pages, D), bf16),
            V((R, pages, D), bf16),
            V((chunks, n, R // chunks * hb, DL), bf16),
            V((n, 2, hb, 128), f32),
            V((chunks, n, R // chunks * hb, DL), bf16),
            V((n, 2, hb, 128), f32),
            V((groups, 128), f32),
            V((hc, groups, 128), f32),
            dma((2 + R,)),
            dma((n,)), dma((n,)),
            dma((chunks, n)), dma((chunks, n)),
            dma((n,)), dma((n,)),
            dma((hc,)), dma((hc,)),
        ],
        compiler_params=pltpu.CompilerParams(
            collective_id=0, has_side_effects=True, vmem_limit_bytes=40 * 1024 * 1024
        ),
    )(lengths, q_nope, q_rope, selected, w_uk, w_uv, cache)


def solution(mesh):
    placed = (
        P("grp", ("seq", "head"), None),
        P("grp", ("seq", "head"), None),
        P(("seq", "head"), None, None),
        P(("seq", "head"), None, None),
        P("grp", "seq", None),
        P("grp"),
        P("grp", None, None),
    )
    return jax.shard_map(
        functools.partial(local, mesh.shape["seq"], mesh.shape["head"]),
        mesh=mesh,
        in_specs=placed,
        out_specs=(P("grp", ("seq", "head"), None), P("grp", None, "seq")),
        check_vma=False,
    )
```

```python
import functools

import jax
import jax.numpy as jnp
from jax import lax
from jax.experimental import pallas as pl
from jax.experimental.pallas import tpu as pltpu
from jax.sharding import PartitionSpec as P

GH = 16
PAGE = 64
LOWEST = -1e30
FLOOR = -1e29
NT = (((1,), (1,)), ((), ()))


def kernel(
    n, hc, R, hb, T, DL, D, groups, scale,
    len_ref, qn_ref, qr_ref, sel_ref, wuk_hbm, wuv_hbm, cache_hbm,
    out_ref, bounds_ref,
    wuk, wuv, cache, gq, qf, pen, hi_s, lo_s, so, st, ro, rs, gb, gbr,
    in_sem, uk_sem, q_send, q_recv, o_send, o_recv, s_send, s_recv, b_send, b_recv,
):
    f32, bf16 = jnp.float32, jnp.bfloat16
    me = lax.axis_index("seq")
    hr = lax.axis_index("head")
    H = n * hb
    chunks = so.shape[0]
    RC = R // chunks
    pages = T // PAGE

    load_uk = [
        pltpu.make_async_copy(wuk_hbm.at[h], wuk.at[h], uk_sem.at[h]) for h in range(hb)
    ]
    load_cache = [
        pltpu.make_async_copy(cache_hbm.at[r], cache.at[r], in_sem.at[2 + r]) for r in range(R)
    ]
    load_uv = pltpu.make_async_copy(wuv_hbm, wuv, in_sem.at[1])
    for c in load_uk:
        c.start()

    barrier = pltpu.get_barrier_semaphore()
    for k in range(1, n):
        pl.semaphore_signal(barrier, inc=1, device_id={"seq": lax.rem(me + k, n)})
    for k in range(1, hc):
        pl.semaphore_signal(barrier, inc=1, device_id={"head": lax.rem(hr + k, hc)})

    def spread(rows, width):
        which = lax.rem(lax.broadcasted_iota(jnp.int32, (R * hb, width), 0), hb)
        return jnp.concatenate(
            [jnp.where(which == h, rows, 0.0).astype(bf16) for h in range(hb)], axis=1
        )

    qn = jnp.concatenate([qn_ref[r].astype(f32) for r in range(R)], axis=0)
    qr = jnp.concatenate([qr_ref[r].astype(f32) for r in range(R)], axis=0)
    lhs = spread(qn, qn.shape[1])
    for c in load_uk:
        c.wait()
    for c in load_cache:
        c.start()
    load_uv.start()
    latent = jnp.dot(lhs, wuk[...].reshape(lhs.shape[1], DL), preferred_element_type=f32)
    RH = RC * hb
    for c in range(chunks):
        gq[c, me, :, :DL] = latent[c * RH:(c + 1) * RH].astype(bf16)
        gq[c, me, :, DL:] = qr[c * RH:(c + 1) * RH].astype(bf16)

    pl.semaphore_wait(barrier, n - 1 + hc - 1)
    q_copies = [[] for _ in range(chunks)]
    for c in range(chunks):
        for k in range(1, n):
            cp = pltpu.make_async_remote_copy(
                src_ref=gq.at[c, me], dst_ref=gq.at[c, me],
                send_sem=q_send.at[c, k], recv_sem=q_recv.at[c, k],
                device_id={"seq": lax.rem(me + k, n)},
            )
            cp.start()
            q_copies[c].append(cp)

    row_head = lax.broadcasted_iota(jnp.int32, (H, groups), 0)
    row_head = (lax.div(row_head, hb) * hc + hr) * hb + lax.rem(row_head, hb)
    hot = lax.div(row_head, GH) == lax.broadcasted_iota(jnp.int32, (H, groups), 1)
    hot_b = jnp.where(hot, 1.0, 0.0).astype(bf16)
    tok = me * T + lax.broadcasted_iota(jnp.int32, (groups, T), 1)
    page_of = lax.div(tok, PAGE)
    tok_col = me * T + lax.broadcasted_iota(jnp.int32, (T, 1), 0)
    page_col = (me * pages + lax.broadcasted_iota(jnp.int32, (pages, 1), 0)) * PAGE
    for r in range(R):
        length = len_ref[r]
        sel = sel_ref[r]
        hit = jnp.zeros((groups, T), f32)
        for k in range(sel.shape[1]):
            hit = jnp.where(sel[:, k:k + 1] == page_of, 1.0, hit)
        hit = jnp.where(tok < length, hit, 0.0)
        mask = jnp.dot(hot_b, hit.astype(bf16), preferred_element_type=f32)
        pen[r] = (1.0 - mask) * LOWEST
    TILE = 128 if T % 128 == 0 else T
    eye = jnp.where(
        lax.broadcasted_iota(jnp.int32, (TILE, TILE), 0)
        == lax.broadcasted_iota(jnp.int32, (TILE, TILE), 1), 1.0, 0.0
    ).astype(bf16)
    for r in range(R):
        length = len_ref[r]
        load_cache[r].wait()
        x = jnp.concatenate(
            [
                lax.dot_general(
                    eye, cache[r, :, t * TILE:(t + 1) * TILE], NT, preferred_element_type=f32
                )
                for t in range(T // TILE)
            ],
            axis=0,
        )
        live = tok_col < length
        low = jnp.min(jnp.where(live, x, jnp.inf).reshape(pages, PAGE, D), axis=1)
        high = jnp.max(jnp.where(live, x, -jnp.inf).reshape(pages, PAGE, D), axis=1)
        live_page = page_col < length
        lo_s[r] = jnp.where(live_page, low, 0.0).astype(bf16)
        hi_s[r] = jnp.where(live_page, high, 0.0).astype(bf16)

    lane = lax.broadcasted_iota(jnp.int32, (H, 128), 1)
    tops = jnp.zeros((H, 128), f32)
    sums = jnp.ones((H, 128), f32)
    o_copies = []
    for c in range(chunks):
        outs = []
        for cp in q_copies[c]:
            cp.wait_recv()
        for b in range(n):
            block = gq[c, b].astype(f32)
            for i in range(RC):
                qf[c * RC + i, b * hb:(b + 1) * hb, :] = block[i * hb:(i + 1) * hb]
        for r in range(c * RC, (c + 1) * RC):
            q = qf[r].astype(bf16)
            s = jnp.dot(q, cache[r], preferred_element_type=f32) * scale + pen[r]
            m = jnp.maximum(jnp.max(s, axis=1, keepdims=True), FLOOR)
            w = jnp.exp(s - m).astype(bf16)
            l = jnp.sum(w.astype(f32), axis=1, keepdims=True)
            outs.append(lax.dot_general(w, cache[r, :DL, :], NT, preferred_element_type=f32))
            tops = jnp.where(lane == r, m, tops)
            sums = jnp.where(lane == r, l, sums)
        for b in range(n):
            so[c, b] = jnp.concatenate(
                [o[b * hb:(b + 1) * hb] for o in outs], axis=0
            ).astype(bf16)
        if c == chunks - 1:
            for b in range(n):
                st[b, 0] = tops[b * hb:(b + 1) * hb]
                st[b, 1] = sums[b * hb:(b + 1) * hb]
        for k in range(1, n):
            to = lax.rem(me + k, n)
            cp = pltpu.make_async_remote_copy(
                src_ref=so.at[c, to], dst_ref=ro.at[c, me],
                send_sem=o_send.at[c, k], recv_sem=o_recv.at[c, k], device_id={"seq": to},
            )
            cp.start()
            o_copies.append(cp)
            if c == chunks - 1:
                cp = pltpu.make_async_remote_copy(
                    src_ref=st.at[to], dst_ref=rs.at[me],
                    send_sem=s_send.at[k], recv_sem=s_recv.at[k], device_id={"seq": to},
                )
                cp.start()
                o_copies.append(cp)

    parts = []
    for r in range(R):
        q = qf[r]
        above = jnp.maximum(q, 0.0).astype(bf16)
        below = jnp.minimum(q, 0.0).astype(bf16)
        parts.append(
            lax.dot_general(above, hi_s[r], NT, preferred_element_type=f32)
            + lax.dot_general(below, lo_s[r], NT, preferred_element_type=f32)
        )
    parts.append(jnp.zeros((H, 128 - R * pages), f32))
    head_bound = jnp.concatenate(parts, axis=1) * scale
    gb[...] = jnp.concatenate(
        [
            jnp.max(jnp.where(hot[:, g:g + 1], head_bound, LOWEST), axis=0, keepdims=True)
            for g in range(groups)
        ],
        axis=0,
    )
    b_copies = []
    for k in range(1, hc):
        cp = pltpu.make_async_remote_copy(
            src_ref=gb, dst_ref=gbr.at[k], send_sem=b_send.at[k], recv_sem=b_recv.at[k],
            device_id={"head": lax.rem(hr + k, hc)},
        )
        cp.start()
        b_copies.append(cp)
    for c in range(chunks):
        ro[c, me] = so[c, me]
    rs[me] = st[me]
    load_uv.wait()
    for cp in b_copies:
        cp.wait_recv()
    best = gb[...]
    for k in range(1, hc):
        best = jnp.maximum(best, gbr[k])
    page_row = (me * pages + lax.broadcasted_iota(jnp.int32, (groups, pages), 1)) * PAGE
    for r in range(R):
        bounds_ref[r] = jnp.where(
            page_row < len_ref[r], best[:, r * pages:(r + 1) * pages], 0.0
        )

    for cp in o_copies:
        cp.wait_recv()
    peak = rs[0, 0]
    for b in range(1, n):
        peak = jnp.maximum(peak, rs[b, 0])
    shares = [jnp.exp(rs[b, 0] - peak) for b in range(n)]
    total = shares[0] * rs[0, 1]
    for b in range(1, n):
        total += shares[b] * rs[b, 1]
    shares = [x / total for x in shares]
    rows = []
    for c in range(chunks):
        acc = [jnp.zeros((hb, DL), f32) for _ in range(RC)]
        for b in range(n):
            block = ro[c, b].astype(f32)
            for i in range(RC):
                r = c * RC + i
                acc[i] += shares[b][:, r:r + 1] * block[i * hb:(i + 1) * hb]
        rows += acc
    lhs = spread(jnp.concatenate(rows, axis=0), DL)
    res = jnp.dot(lhs, wuv[...].reshape(lhs.shape[1], wuv.shape[2]), preferred_element_type=f32)
    for r in range(R):
        out_ref[r] = res[r * hb:(r + 1) * hb].astype(bf16)
    for cp in sum(q_copies, []) + o_copies + b_copies:
        cp.wait_send()


def local(n, hc, q_nope, q_rope, w_uk, w_uv, cache, lengths, selected):
    R, hb, DN = q_nope.shape
    DL, DV = w_uk.shape[2], w_uv.shape[2]
    T, D = cache.shape[1:]
    groups = selected.shape[1]
    pages = T // PAGE
    H = n * hb
    chunks = 2 if R % 2 == 0 else 1
    scale = (DN + q_rope.shape[2]) ** (-0.5)
    f32, bf16 = jnp.float32, jnp.bfloat16
    V = pltpu.VMEM
    vm = pl.BlockSpec(memory_space=pltpu.VMEM)
    hbm = pl.BlockSpec(memory_space=pl.ANY)
    dma = pltpu.SemaphoreType.DMA
    return pl.pallas_call(
        functools.partial(kernel, n, hc, R, hb, T, DL, D, groups, scale),
        out_shape=(
            jax.ShapeDtypeStruct((R, hb, DV), bf16),
            jax.ShapeDtypeStruct((R, groups, pages), f32),
        ),
        in_specs=[pl.BlockSpec(memory_space=pltpu.SMEM), vm, vm, vm, hbm, hbm, hbm],
        out_specs=(vm, vm),
        scratch_shapes=[
            V((hb, DN, DL), bf16),
            V((hb, DL, DV), bf16),
            V((R, D, T), bf16),
            V((chunks, n, R // chunks * hb, D), bf16),
            V((R, H, D), f32),
            V((R, H, T), f32),
            V((R, pages, D), bf16),
            V((R, pages, D), bf16),
            V((chunks, n, R // chunks * hb, DL), bf16),
            V((n, 2, hb, 128), f32),
            V((chunks, n, R // chunks * hb, DL), bf16),
            V((n, 2, hb, 128), f32),
            V((groups, 128), f32),
            V((hc, groups, 128), f32),
            dma((2 + R,)),
            dma((hb,)),
            dma((chunks, n)), dma((chunks, n)),
            dma((chunks, n)), dma((chunks, n)),
            dma((n,)), dma((n,)),
            dma((hc,)), dma((hc,)),
        ],
        compiler_params=pltpu.CompilerParams(
            collective_id=0, has_side_effects=True
        ),
    )(lengths, q_nope, q_rope, selected, w_uk, w_uv, jnp.swapaxes(cache, 1, 2))


def solution(mesh):
    placed = (
        P("grp", ("seq", "head"), None),
        P("grp", ("seq", "head"), None),
        P(("seq", "head"), None, None),
        P(("seq", "head"), None, None),
        P("grp", "seq", None),
        P("grp"),
        P("grp", None, None),
    )
    return jax.shard_map(
        functools.partial(local, mesh.shape["seq"], mesh.shape["head"]),
        mesh=mesh,
        in_specs=placed,
        out_specs=(P("grp", ("seq", "head"), None), P("grp", None, "seq")),
        check_vma=False,
    )
```

```python
import functools

import jax
import jax.numpy as jnp
from jax import lax
from jax.experimental import pallas as pl
from jax.experimental.pallas import tpu as pltpu
from jax.sharding import PartitionSpec as P

GH = 16
PAGE = 64
LOWEST = -1e30
FLOOR = -1e29
NT = (((1,), (1,)), ((), ()))


def kernel(
    n, hc, R, hb, T, DL, D, groups, scale,
    len_ref, qn_ref, qr_ref, sel_ref, wuk_hbm, wuv_hbm, cache_hbm,
    out_ref, bounds_ref,
    wuk, wuv, cache, gq, qf, pen, hi_s, lo_s, so, st, ro, rs, gb, gbr,
    in_sem, uk_sem, q_send, q_recv, o_send, o_recv, s_send, s_recv, b_send, b_recv,
):
    f32, bf16 = jnp.float32, jnp.bfloat16
    me = lax.axis_index("seq")
    hr = lax.axis_index("head")
    H = n * hb
    chunks = so.shape[0]
    RC = R // chunks
    pages = T // PAGE

    load_uk = [
        pltpu.make_async_copy(wuk_hbm.at[h], wuk.at[h], uk_sem.at[h]) for h in range(hb)
    ]
    load_cache = [
        pltpu.make_async_copy(cache_hbm.at[r], cache.at[r], in_sem.at[2 + r]) for r in range(R)
    ]
    load_uv = pltpu.make_async_copy(wuv_hbm, wuv, in_sem.at[1])
    for c in load_uk:
        c.start()

    barrier = pltpu.get_barrier_semaphore()
    for k in range(1, n):
        pl.semaphore_signal(barrier, inc=1, device_id={"seq": lax.rem(me + k, n)})
    for k in range(1, hc):
        pl.semaphore_signal(barrier, inc=1, device_id={"head": lax.rem(hr + k, hc)})

    def spread(rows, width):
        which = lax.rem(lax.broadcasted_iota(jnp.int32, (R * hb, width), 0), hb)
        return jnp.concatenate(
            [jnp.where(which == h, rows, 0.0).astype(bf16) for h in range(hb)], axis=1
        )

    qn = jnp.concatenate([qn_ref[r].astype(f32) for r in range(R)], axis=0)
    qr = jnp.concatenate([qr_ref[r].astype(f32) for r in range(R)], axis=0)
    lhs = spread(qn, qn.shape[1])
    for c in load_uk:
        c.wait()
    for c in load_cache:
        c.start()
    load_uv.start()
    latent = jnp.dot(lhs, wuk[...].reshape(lhs.shape[1], DL), preferred_element_type=f32)
    RH = RC * hb
    for c in range(chunks):
        gq[c, me, :, :DL] = latent[c * RH:(c + 1) * RH].astype(bf16)
        gq[c, me, :, DL:] = qr[c * RH:(c + 1) * RH].astype(bf16)

    pl.semaphore_wait(barrier, n - 1 + hc - 1)
    step = 2 if n % 2 == 0 else 1
    pair = me + 1 - 2 * lax.rem(me, 2)

    def query_copy(c, slot, k, to):
        return pltpu.make_async_remote_copy(
            src_ref=gq.at[c, slot], dst_ref=gq.at[c, slot],
            send_sem=q_send.at[c, k], recv_sem=q_recv.at[c, k], device_id={"seq": to},
        )

    far_first = sorted(range(1, n), key=lambda k: -min(k, n - k))
    evens = [k for k in far_first if k % step == 0]
    direct = [[] for _ in range(chunks)]
    passed = [[] for _ in range(chunks)]
    for c in range(chunks):
        for k in evens:
            cp = query_copy(c, me, k, lax.rem(me + k, n))
            cp.start()
            direct[c].append(cp)
        if step == 2:
            cp = query_copy(c, me, 1, pair)
            cp.start()
            passed[c].append(cp)

    row_head = lax.broadcasted_iota(jnp.int32, (H, groups), 0)
    row_head = (lax.div(row_head, hb) * hc + hr) * hb + lax.rem(row_head, hb)
    hot = lax.div(row_head, GH) == lax.broadcasted_iota(jnp.int32, (H, groups), 1)
    hot_b = jnp.where(hot, 1.0, 0.0).astype(bf16)
    tok = me * T + lax.broadcasted_iota(jnp.int32, (groups, T), 1)
    page_of = lax.div(tok, PAGE)
    tok_col = me * T + lax.broadcasted_iota(jnp.int32, (T, 1), 0)
    page_col = (me * pages + lax.broadcasted_iota(jnp.int32, (pages, 1), 0)) * PAGE
    for r in range(R):
        length = len_ref[r]
        sel = sel_ref[r]
        hit = jnp.zeros((groups, T), f32)
        for k in range(sel.shape[1]):
            hit = jnp.where(sel[:, k:k + 1] == page_of, 1.0, hit)
        hit = jnp.where(tok < length, hit, 0.0)
        mask = jnp.dot(hot_b, hit.astype(bf16), preferred_element_type=f32)
        pen[r] = (1.0 - mask) * LOWEST
    if step == 2:
        for c in range(chunks):
            for i in reversed(range(len(evens))):
                k = evens[i]
                direct[c][i].wait_recv()
                cp = query_copy(c, lax.rem(me + n - k, n), k + 1, pair)
                cp.start()
                passed[c].append(cp)

    lane = lax.broadcasted_iota(jnp.int32, (H, 128), 1)
    tops = jnp.zeros((H, 128), f32)
    sums = jnp.ones((H, 128), f32)
    o_copies = []
    for c in range(chunks):
        outs = []
        for cp in passed[c] if step == 2 else direct[c]:
            cp.wait_recv()
        for b in range(n):
            block = gq[c, b].astype(f32)
            for i in range(RC):
                qf[c * RC + i, b * hb:(b + 1) * hb, :] = block[i * hb:(i + 1) * hb]
        for r in range(c * RC, (c + 1) * RC):
            q = qf[r].astype(bf16)
            load_cache[r].wait()
            s = jnp.dot(q, cache[r], preferred_element_type=f32) * scale + pen[r]
            m = jnp.maximum(jnp.max(s, axis=1, keepdims=True), FLOOR)
            w = jnp.exp(s - m).astype(bf16)
            l = jnp.sum(w.astype(f32), axis=1, keepdims=True)
            outs.append(lax.dot_general(w, cache[r, :DL, :], NT, preferred_element_type=f32))
            tops = jnp.where(lane == r, m, tops)
            sums = jnp.where(lane == r, l, sums)
        for b in range(n):
            so[c, b] = jnp.concatenate(
                [o[b * hb:(b + 1) * hb] for o in outs], axis=0
            ).astype(bf16)
        if c == chunks - 1:
            for b in range(n):
                st[b, 0] = tops[b * hb:(b + 1) * hb]
                st[b, 1] = sums[b * hb:(b + 1) * hb]
        for k in far_first:
            to = lax.rem(me + k, n)
            cp = pltpu.make_async_remote_copy(
                src_ref=so.at[c, to], dst_ref=ro.at[c, me],
                send_sem=o_send.at[c, k], recv_sem=o_recv.at[c, k], device_id={"seq": to},
            )
            cp.start()
            o_copies.append(cp)
            if c == chunks - 1:
                cp = pltpu.make_async_remote_copy(
                    src_ref=st.at[to], dst_ref=rs.at[me],
                    send_sem=s_send.at[k], recv_sem=s_recv.at[k], device_id={"seq": to},
                )
                cp.start()
                o_copies.append(cp)

    TILE = 128 if T % 128 == 0 else T
    eye = jnp.where(
        lax.broadcasted_iota(jnp.int32, (TILE, TILE), 0)
        == lax.broadcasted_iota(jnp.int32, (TILE, TILE), 1), 1.0, 0.0
    ).astype(bf16)
    for r in range(R):
        length = len_ref[r]
        x = jnp.concatenate(
            [
                lax.dot_general(
                    eye, cache[r, :, t * TILE:(t + 1) * TILE], NT, preferred_element_type=f32
                )
                for t in range(T // TILE)
            ],
            axis=0,
        )
        live = tok_col < length
        low = jnp.min(jnp.where(live, x, jnp.inf).reshape(pages, PAGE, D), axis=1)
        high = jnp.max(jnp.where(live, x, -jnp.inf).reshape(pages, PAGE, D), axis=1)
        live_page = page_col < length
        lo_s[r] = jnp.where(live_page, low, 0.0).astype(bf16)
        hi_s[r] = jnp.where(live_page, high, 0.0).astype(bf16)

    parts = []
    for r in range(R):
        q = qf[r]
        above = jnp.maximum(q, 0.0).astype(bf16)
        below = jnp.minimum(q, 0.0).astype(bf16)
        parts.append(
            lax.dot_general(above, hi_s[r], NT, preferred_element_type=f32)
            + lax.dot_general(below, lo_s[r], NT, preferred_element_type=f32)
        )
    parts.append(jnp.zeros((H, 128 - R * pages), f32))
    head_bound = jnp.concatenate(parts, axis=1) * scale
    gb[...] = jnp.concatenate(
        [
            jnp.max(jnp.where(hot[:, g:g + 1], head_bound, LOWEST), axis=0, keepdims=True)
            for g in range(groups)
        ],
        axis=0,
    )
    b_copies = []
    for k in range(1, hc):
        cp = pltpu.make_async_remote_copy(
            src_ref=gb, dst_ref=gbr.at[k], send_sem=b_send.at[k], recv_sem=b_recv.at[k],
            device_id={"head": lax.rem(hr + k, hc)},
        )
        cp.start()
        b_copies.append(cp)
    for c in range(chunks):
        ro[c, me] = so[c, me]
    rs[me] = st[me]
    load_uv.wait()
    for cp in b_copies:
        cp.wait_recv()
    best = gb[...]
    for k in range(1, hc):
        best = jnp.maximum(best, gbr[k])
    page_row = (me * pages + lax.broadcasted_iota(jnp.int32, (groups, pages), 1)) * PAGE
    for r in range(R):
        bounds_ref[r] = jnp.where(
            page_row < len_ref[r], best[:, r * pages:(r + 1) * pages], 0.0
        )

    for cp in o_copies:
        cp.wait_recv()
    peak = rs[0, 0]
    for b in range(1, n):
        peak = jnp.maximum(peak, rs[b, 0])
    shares = [jnp.exp(rs[b, 0] - peak) for b in range(n)]
    total = shares[0] * rs[0, 1]
    for b in range(1, n):
        total += shares[b] * rs[b, 1]
    shares = [x / total for x in shares]
    rows = []
    for c in range(chunks):
        acc = [jnp.zeros((hb, DL), f32) for _ in range(RC)]
        for b in range(n):
            block = ro[c, b].astype(f32)
            for i in range(RC):
                r = c * RC + i
                acc[i] += shares[b][:, r:r + 1] * block[i * hb:(i + 1) * hb]
        rows += acc
    lhs = spread(jnp.concatenate(rows, axis=0), DL)
    res = jnp.dot(lhs, wuv[...].reshape(lhs.shape[1], wuv.shape[2]), preferred_element_type=f32)
    for r in range(R):
        out_ref[r] = res[r * hb:(r + 1) * hb].astype(bf16)
    for cp in sum(direct + passed, []) + o_copies + b_copies:
        cp.wait_send()


def local(n, hc, q_nope, q_rope, w_uk, w_uv, cache, lengths, selected):
    R, hb, DN = q_nope.shape
    DL, DV = w_uk.shape[2], w_uv.shape[2]
    T, D = cache.shape[1:]
    groups = selected.shape[1]
    pages = T // PAGE
    H = n * hb
    chunks = 2 if R % 2 == 0 else 1
    scale = (DN + q_rope.shape[2]) ** (-0.5)
    f32, bf16 = jnp.float32, jnp.bfloat16
    V = pltpu.VMEM
    vm = pl.BlockSpec(memory_space=pltpu.VMEM)
    hbm = pl.BlockSpec(memory_space=pltpu.HBM)
    dma = pltpu.SemaphoreType.DMA
    return pl.pallas_call(
        functools.partial(kernel, n, hc, R, hb, T, DL, D, groups, scale),
        out_shape=(
            V((R, hb, DV), bf16),
            V((R, groups, pages), f32),
        ),
        in_specs=[pl.BlockSpec(memory_space=pltpu.SMEM), vm, vm, vm, hbm, hbm, hbm],
        out_specs=(vm, vm),
        scratch_shapes=[
            V((hb, DN, DL), bf16),
            V((hb, DL, DV), bf16),
            V((R, D, T), bf16),
            V((chunks, n, R // chunks * hb, D), bf16),
            V((R, H, D), f32),
            V((R, H, T), f32),
            V((R, pages, D), bf16),
            V((R, pages, D), bf16),
            V((chunks, n, R // chunks * hb, DL), bf16),
            V((n, 2, hb, 128), f32),
            V((chunks, n, R // chunks * hb, DL), bf16),
            V((n, 2, hb, 128), f32),
            V((groups, 128), f32),
            V((hc, groups, 128), f32),
            dma((2 + R,)),
            dma((hb,)),
            dma((chunks, n)), dma((chunks, n)),
            dma((chunks, n)), dma((chunks, n)),
            dma((n,)), dma((n,)),
            dma((hc,)), dma((hc,)),
        ],
        compiler_params=pltpu.CompilerParams(
            collective_id=0, has_side_effects=True, vmem_limit_bytes=61000 * 1024
        ),
    )(lengths, q_nope, q_rope, selected, w_uk, w_uv, jnp.swapaxes(cache, 1, 2))


def solution(mesh):
    placed = (
        P("grp", ("seq", "head"), None),
        P("grp", ("seq", "head"), None),
        P(("seq", "head"), None, None),
        P(("seq", "head"), None, None),
        P("grp", "seq", None),
        P("grp"),
        P("grp", None, None),
    )
    return jax.shard_map(
        functools.partial(local, mesh.shape["seq"], mesh.shape["head"]),
        mesh=mesh,
        in_specs=placed,
        out_specs=(P("grp", ("seq", "head"), None), P("grp", None, "seq")),
        check_vma=False,
    )
```

```python
import functools

import jax
import jax.numpy as jnp
from jax import lax
from jax.experimental import pallas as pl
from jax.experimental.pallas import tpu as pltpu
from jax.sharding import PartitionSpec as P

GH = 16
PAGE = 64
LOWEST = -1e30
FLOOR = -1e29
NT = (((1,), (1,)), ((), ()))


def kernel(
    n, hc, R, hb, T, DL, D, groups, scale,
    len_ref, qn_ref, qr_ref, sel_ref, wuk_hbm, wuv_hbm, cache_hbm,
    out_ref, bounds_ref,
    wuk, wuv, cache, gq, qf, pen, hi_s, lo_s, so, st, ro, rs, gb, gbr,
    in_sem, uk_sem, q_send, q_recv, o_send, o_recv, s_send, s_recv, b_send, b_recv,
):
    f32, bf16 = jnp.float32, jnp.bfloat16
    me = lax.axis_index("seq")
    hr = lax.axis_index("head")
    H = n * hb
    chunks = so.shape[0]
    RC = R // chunks
    pages = T // PAGE

    load_uk = [
        pltpu.make_async_copy(wuk_hbm.at[h], wuk.at[h], uk_sem.at[h]) for h in range(hb)
    ]
    load_cache = [
        pltpu.make_async_copy(cache_hbm.at[r], cache.at[r], in_sem.at[2 + r]) for r in range(R)
    ]
    load_uv = pltpu.make_async_copy(wuv_hbm, wuv, in_sem.at[1])
    for c in load_uk:
        c.start()

    barrier = pltpu.get_barrier_semaphore()
    for k in range(1, n):
        pl.semaphore_signal(barrier, inc=1, device_id={"seq": lax.rem(me + k, n)})
    for k in range(1, hc):
        pl.semaphore_signal(barrier, inc=1, device_id={"head": lax.rem(hr + k, hc)})

    def spread(rows, width):
        which = lax.rem(lax.broadcasted_iota(jnp.int32, (R * hb, width), 0), hb)
        return jnp.concatenate(
            [jnp.where(which == h, rows, 0.0).astype(bf16) for h in range(hb)], axis=1
        )

    qn = jnp.concatenate([qn_ref[r].astype(f32) for r in range(R)], axis=0)
    qr = jnp.concatenate([qr_ref[r].astype(f32) for r in range(R)], axis=0)
    lhs = spread(qn, qn.shape[1])
    for c in load_uk:
        c.wait()
    for c in load_cache:
        c.start()
    load_uv.start()
    latent = jnp.dot(lhs, wuk[...].reshape(lhs.shape[1], DL), preferred_element_type=f32)
    RH = RC * hb
    for c in range(chunks):
        gq[c, me, :, :DL] = latent[c * RH:(c + 1) * RH].astype(bf16)
        gq[c, me, :, DL:] = qr[c * RH:(c + 1) * RH].astype(bf16)

    pl.semaphore_wait(barrier, n - 1 + hc - 1)
    step = 2 if n % 2 == 0 else 1
    pair = me + 1 - 2 * lax.rem(me, 2)

    def query_copy(c, slot, k, to):
        return pltpu.make_async_remote_copy(
            src_ref=gq.at[c, slot], dst_ref=gq.at[c, slot],
            send_sem=q_send.at[c, k], recv_sem=q_recv.at[c, k], device_id={"seq": to},
        )

    far_first = sorted(range(1, n), key=lambda k: -min(k, n - k))
    evens = [k for k in far_first if k % step == 0]
    direct = [[] for _ in range(chunks)]
    passed = [[] for _ in range(chunks)]
    for c in range(chunks):
        for k in evens:
            cp = query_copy(c, me, k, lax.rem(me + k, n))
            cp.start()
            direct[c].append(cp)
        if step == 2:
            cp = query_copy(c, me, 1, pair)
            cp.start()
            passed[c].append(cp)

    row_head = lax.broadcasted_iota(jnp.int32, (H, groups), 0)
    row_head = (lax.div(row_head, hb) * hc + hr) * hb + lax.rem(row_head, hb)
    hot = lax.div(row_head, GH) == lax.broadcasted_iota(jnp.int32, (H, groups), 1)
    hot_b = jnp.where(hot, 1.0, 0.0).astype(bf16)
    tok = me * T + lax.broadcasted_iota(jnp.int32, (groups, T), 1)
    page_of = lax.div(tok, PAGE)
    tok_col = me * T + lax.broadcasted_iota(jnp.int32, (T, 1), 0)
    page_col = (me * pages + lax.broadcasted_iota(jnp.int32, (pages, 1), 0)) * PAGE
    for r in range(R):
        length = len_ref[r]
        sel = sel_ref[r]
        hit = jnp.zeros((groups, T), f32)
        for k in range(sel.shape[1]):
            hit = jnp.where(sel[:, k:k + 1] == page_of, 1.0, hit)
        hit = jnp.where(tok < length, hit, 0.0)
        mask = jnp.dot(hot_b, hit.astype(bf16), preferred_element_type=f32)
        pen[r] = (1.0 - mask) * LOWEST
    if step == 2:
        for c in range(chunks):
            for i in reversed(range(len(evens))):
                k = evens[i]
                direct[c][i].wait_recv()
                cp = query_copy(c, lax.rem(me + n - k, n), k + 1, pair)
                cp.start()
                passed[c].append(cp)

    lane = lax.broadcasted_iota(jnp.int32, (H, 128), 1)
    HALF = 64
    stats = jnp.where(lane < HALF, 0.0, 1.0)
    o_copies = []
    for c in range(chunks):
        outs = []
        for cp in passed[c] if step == 2 else direct[c]:
            cp.wait_recv()
        for b in range(n):
            block = gq[c, b].astype(f32)
            for i in range(RC):
                qf[c * RC + i, b * hb:(b + 1) * hb, :] = block[i * hb:(i + 1) * hb]
        for r in range(c * RC, (c + 1) * RC):
            q = qf[r].astype(bf16)
            load_cache[r].wait()
            s = jnp.dot(q, cache[r], preferred_element_type=f32) * scale + pen[r]
            m = jnp.maximum(jnp.max(s, axis=1, keepdims=True), FLOOR)
            w = jnp.exp(s - m).astype(bf16)
            l = jnp.sum(w.astype(f32), axis=1, keepdims=True)
            outs.append(lax.dot_general(w, cache[r, :DL, :], NT, preferred_element_type=f32))
            stats = jnp.where(lane == r, m, jnp.where(lane == HALF + r, l, stats))
        for b in range(n):
            so[c, b] = jnp.concatenate(
                [o[b * hb:(b + 1) * hb] for o in outs], axis=0
            ).astype(bf16)
        if c == chunks - 1:
            for b in range(n):
                st[b] = stats[b * hb:(b + 1) * hb]
        for k in far_first:
            to = lax.rem(me + k, n)
            cp = pltpu.make_async_remote_copy(
                src_ref=so.at[c, to], dst_ref=ro.at[c, me],
                send_sem=o_send.at[c, k], recv_sem=o_recv.at[c, k], device_id={"seq": to},
            )
            cp.start()
            o_copies.append(cp)
            if c == chunks - 1:
                cp = pltpu.make_async_remote_copy(
                    src_ref=st.at[to], dst_ref=rs.at[me],
                    send_sem=s_send.at[k], recv_sem=s_recv.at[k], device_id={"seq": to},
                )
                cp.start()
                o_copies.append(cp)

    TILE = 128 if T % 128 == 0 else T
    eye = jnp.where(
        lax.broadcasted_iota(jnp.int32, (TILE, TILE), 0)
        == lax.broadcasted_iota(jnp.int32, (TILE, TILE), 1), 1.0, 0.0
    ).astype(bf16)
    for r in range(R):
        length = len_ref[r]
        x = jnp.concatenate(
            [
                lax.dot_general(
                    eye, cache[r, :, t * TILE:(t + 1) * TILE], NT, preferred_element_type=f32
                )
                for t in range(T // TILE)
            ],
            axis=0,
        )
        live = tok_col < length
        low = jnp.min(jnp.where(live, x, jnp.inf).reshape(pages, PAGE, D), axis=1)
        high = jnp.max(jnp.where(live, x, -jnp.inf).reshape(pages, PAGE, D), axis=1)
        live_page = page_col < length
        lo_s[r] = jnp.where(live_page, low, 0.0).astype(bf16)
        hi_s[r] = jnp.where(live_page, high, 0.0).astype(bf16)

    parts = []
    for r in range(R):
        q = qf[r]
        above = jnp.maximum(q, 0.0).astype(bf16)
        below = jnp.minimum(q, 0.0).astype(bf16)
        parts.append(
            lax.dot_general(above, hi_s[r], NT, preferred_element_type=f32)
            + lax.dot_general(below, lo_s[r], NT, preferred_element_type=f32)
        )
    parts.append(jnp.zeros((H, 128 - R * pages), f32))
    head_bound = jnp.concatenate(parts, axis=1) * scale
    gb[...] = jnp.concatenate(
        [
            jnp.max(jnp.where(hot[:, g:g + 1], head_bound, LOWEST), axis=0, keepdims=True)
            for g in range(groups)
        ],
        axis=0,
    )
    b_copies = []
    for k in range(1, hc):
        cp = pltpu.make_async_remote_copy(
            src_ref=gb, dst_ref=gbr.at[k], send_sem=b_send.at[k], recv_sem=b_recv.at[k],
            device_id={"head": lax.rem(hr + k, hc)},
        )
        cp.start()
        b_copies.append(cp)
    for c in range(chunks):
        ro[c, me] = so[c, me]
    rs[me] = st[me]
    load_uv.wait()
    for cp in b_copies:
        cp.wait_recv()
    best = gb[...]
    for k in range(1, hc):
        best = jnp.maximum(best, gbr[k])
    page_row = (me * pages + lax.broadcasted_iota(jnp.int32, (groups, pages), 1)) * PAGE
    for r in range(R):
        bounds_ref[r] = jnp.where(
            page_row < len_ref[r], best[:, r * pages:(r + 1) * pages], 0.0
        )

    for cp in o_copies:
        cp.wait_recv()
    peak = rs[0]
    for b in range(1, n):
        peak = jnp.maximum(peak, rs[b])
    shares = [jnp.exp(rs[b] - peak) for b in range(n)]
    total = shares[0] * pltpu.roll(rs[0], HALF, 1)
    for b in range(1, n):
        total += shares[b] * pltpu.roll(rs[b], HALF, 1)
    shares = [x / total for x in shares]
    rows = []
    for c in range(chunks):
        acc = [jnp.zeros((hb, DL), f32) for _ in range(RC)]
        for b in range(n):
            block = ro[c, b].astype(f32)
            for i in range(RC):
                r = c * RC + i
                acc[i] += shares[b][:, r:r + 1] * block[i * hb:(i + 1) * hb]
        rows += acc
    lhs = spread(jnp.concatenate(rows, axis=0), DL)
    res = jnp.dot(lhs, wuv[...].reshape(lhs.shape[1], wuv.shape[2]), preferred_element_type=f32)
    for r in range(R):
        out_ref[r] = res[r * hb:(r + 1) * hb].astype(bf16)
    for cp in sum(direct + passed, []) + o_copies + b_copies:
        cp.wait_send()


def local(n, hc, q_nope, q_rope, w_uk, w_uv, cache, lengths, selected):
    R, hb, DN = q_nope.shape
    DL, DV = w_uk.shape[2], w_uv.shape[2]
    T, D = cache.shape[1:]
    groups = selected.shape[1]
    pages = T // PAGE
    H = n * hb
    chunks = R
    scale = (DN + q_rope.shape[2]) ** (-0.5)
    f32, bf16 = jnp.float32, jnp.bfloat16
    V = pltpu.VMEM
    vm = pl.BlockSpec(memory_space=pltpu.VMEM)
    hbm = pl.BlockSpec(memory_space=pltpu.HBM)
    dma = pltpu.SemaphoreType.DMA
    return pl.pallas_call(
        functools.partial(kernel, n, hc, R, hb, T, DL, D, groups, scale),
        out_shape=(
            V((R, hb, DV), bf16),
            V((R, groups, pages), f32),
        ),
        in_specs=[pl.BlockSpec(memory_space=pltpu.SMEM), vm, vm, vm, hbm, hbm, hbm],
        out_specs=(vm, vm),
        scratch_shapes=[
            V((hb, DN, DL), bf16),
            V((hb, DL, DV), bf16),
            V((R, D, T), bf16),
            V((chunks, n, R // chunks * hb, D), bf16),
            V((R, H, D), f32),
            V((R, H, T), f32),
            V((R, pages, D), bf16),
            V((R, pages, D), bf16),
            V((chunks, n, R // chunks * hb, DL), bf16),
            V((n, hb, 128), f32),
            V((chunks, n, R // chunks * hb, DL), bf16),
            V((n, hb, 128), f32),
            V((groups, 128), f32),
            V((hc, groups, 128), f32),
            dma((2 + R,)),
            dma((hb,)),
            dma((chunks, n)), dma((chunks, n)),
            dma((chunks, n)), dma((chunks, n)),
            dma((n,)), dma((n,)),
            dma((hc,)), dma((hc,)),
        ],
        compiler_params=pltpu.CompilerParams(
            collective_id=0, has_side_effects=True, vmem_limit_bytes=61000 * 1024
        ),
    )(lengths, q_nope, q_rope, selected, w_uk, w_uv, jnp.swapaxes(cache, 1, 2))


def solution(mesh):
    placed = (
        P("grp", ("seq", "head"), None),
        P("grp", ("seq", "head"), None),
        P(("seq", "head"), None, None),
        P(("seq", "head"), None, None),
        P("grp", "seq", None),
        P("grp"),
        P("grp", None, None),
    )
    return jax.shard_map(
        functools.partial(local, mesh.shape["seq"], mesh.shape["head"]),
        mesh=mesh,
        in_specs=placed,
        out_specs=(P("grp", ("seq", "head"), None), P("grp", None, "seq")),
        check_vma=False,
    )
```
